32 devices in a mesh: stream: 4 (over x, core), tm: 8 (over z, y).
Axes of the slice: x: 2, y: 2, z: 4, core: 2. Of those that a mesh axis runs over, the one named last changes fastest.
Arguments:
- frames_in: bfloat16 [8, 3072, 1024], P('stream', 'tm'), may hold values from -45 to 45
- w_qkv: bfloat16 [1024, 3072], replicated, may hold values from -1 to 1
- grad_out: bfloat16 [8, 3072, 1024], P('stream', 'tm'), may hold values from -6 to 6
Outputs:
- grad_in: bfloat16 [8, 3072, 1024], P('stream', 'tm')
- grad_w: float32 [1024, 3072], P(('stream', 'tm'))
The draws below stay inside these ranges and needn't reach their ends.
All inputs are finite; a program needn't handle non-finite values.
Results may differ from the reference program's by a relative error of at most 0.015.
Values may be sent and summed in bfloat16 or wider, within the bound.
A program may use at most 192 MiB of HBM per device.

```python
import jax
import jax.numpy as jnp
from jax import lax

D = 1024
HEADS = 8
F_DEV = 384
RECORDINGS = 8
FRAMES = 3072


def draw_frames_in(key, part):
    keys = jax.random.split(key, 1)
    base = jax.random.truncated_normal(keys[0], -4.0, 4.0, (RECORDINGS, FRAMES, D), jnp.float32)
    return base.astype(jnp.bfloat16)


def draw_w_qkv(key, part):
    keys = jax.random.split(key, 1)
    weights = jax.random.truncated_normal(keys[0], -5.0, 5.0, (D, 3 * D), jnp.float32) * D ** (-0.5)
    return weights.astype(jnp.bfloat16)


def shard_levels(rng, shape, pieces, least, largest):
    def one(dim, parts):
        heights = jax.random.uniform(jax.random.fold_in(jax.random.fold_in(rng, 6), dim), (parts,), jnp.float32, least / len(pieces), largest / len(pieces))
        return jnp.repeat(jnp.exp(heights), shape[dim] // parts).reshape((-1,) + (1,) * (len(shape) - dim - 1))

    factor_of = one(*pieces[0])
    for cut in pieces[1:]:
        factor_of = factor_of * one(*cut)
    return factor_of


def normal_values(rng, shape, spread, limit, cuts=(), held_as=jnp.bfloat16):
    entries = spread * jax.random.normal(rng, shape, jnp.float32)
    if cuts:
        entries = entries * shard_levels(rng, shape, cuts, -0.22, 0.18)
    return jnp.clip(entries, -limit, limit).astype(held_as)


def setup_inputs(seed: int = 0) -> dict:
    arg_keys = jax.random.split(jax.random.key(seed), 4)
    return {
        "frames_in": draw_frames_in(jax.random.fold_in(arg_keys[3], 71), 0),
        "w_qkv": draw_w_qkv(jax.random.fold_in(arg_keys[3], 71), 0),
        "grad_out": normal_values(arg_keys[2], (RECORDINGS, FRAMES, D), 1.0, 6.0, ((0, 4), (1, 8))),
    }


def reference(frames_in, w_qkv, grad_out):
    records, frame_count, model_width = frames_in.shape
    head_size = model_width // HEADS
    blocks = frame_count // F_DEV
    score_scale = head_size ** -0.5
    hp = lax.Precision.HIGHEST

    def one_record(pair):
        frames_one, grad_one = pair
        qkv = jnp.dot(frames_one, w_qkv, preferred_element_type=jnp.float32).astype(jnp.bfloat16)
        query_heads = qkv[:, :model_width].reshape(blocks, F_DEV, HEADS, head_size).astype(jnp.float32)
        key_value = qkv[:, model_width:].reshape(blocks, F_DEV, 2 * model_width)
        previous = jnp.concatenate([jnp.zeros_like(key_value[:1]), key_value[:-1]], 0)
        kv_all = jnp.concatenate([previous, key_value], 1).astype(jnp.float32)
        key_heads = kv_all[..., :model_width].reshape(blocks, 2 * F_DEV, HEADS, head_size)
        value_heads = kv_all[..., model_width:].reshape(blocks, 2 * F_DEV, HEADS, head_size)
        scores = jnp.einsum("bfhd,bghd->bhfg", query_heads, key_heads, precision=hp) * score_scale
        block_ids = jnp.arange(blocks)
        columns = jnp.arange(2 * F_DEV)
        valid = jnp.logical_or((block_ids > 0)[:, None, None, None], (columns >= F_DEV)[None, None, None, :])
        scores = jnp.where(valid, scores, -1e30)
        peak = jnp.max(scores, axis=-1, keepdims=True)
        expo = jnp.exp(scores - peak)
        prob = expo / jnp.sum(expo, axis=-1, keepdims=True)
        prob_b = lax.optimization_barrier(prob.astype(jnp.bfloat16)).astype(jnp.float32)
        grad_heads = grad_one.reshape(blocks, F_DEV, HEADS, head_size).astype(jnp.float32)
        dprob = jnp.einsum("bfhd,bghd->bhfg", grad_heads, value_heads, precision=hp)
        delta = jnp.sum(prob * dprob, axis=-1, keepdims=True)
        dscore = lax.optimization_barrier((prob * (dprob - delta) * score_scale).astype(jnp.bfloat16)).astype(jnp.float32)
        grad_query = jnp.einsum("bhfg,bghd->bfhd", dscore, key_heads, precision=hp).astype(jnp.bfloat16)
        grad_key = jnp.einsum("bhfg,bfhd->bghd", dscore, query_heads, precision=hp)
        grad_value = jnp.einsum("bhfg,bfhd->bghd", prob_b, grad_heads, precision=hp)
        grad_kv = jnp.concatenate([grad_key.reshape(blocks, 2 * F_DEV, model_width), grad_value.reshape(blocks, 2 * F_DEV, model_width)], -1)
        earlier = grad_kv[:, :F_DEV]
        own_part = grad_kv[:, F_DEV:]
        summed = own_part + jnp.concatenate([earlier[1:], jnp.zeros_like(earlier[:1])], 0)
        grad_cat = jnp.concatenate([grad_query.reshape(frame_count, model_width), summed.astype(jnp.bfloat16).reshape(frame_count, 2 * model_width)], -1)
        grad_frames = jnp.dot(grad_cat, w_qkv.T, preferred_element_type=jnp.float32).astype(jnp.bfloat16)
        weight_part = jnp.dot(frames_one.T, grad_cat, preferred_element_type=jnp.float32)
        return grad_frames, weight_part

    grad_in, weight_parts = lax.map(one_record, (frames_in, grad_out))
    grad_w = jnp.sum(weight_parts, axis=0) * float(records * frame_count) ** -0.5
    return grad_in, grad_w
```

```python
import functools

import jax
import jax.numpy as jnp
from jax import lax
from jax.experimental import pallas as pl
from jax.experimental.pallas import tpu as pltpu
from jax.sharding import PartitionSpec as P

HEADS = 8
TOGETHER = 2
GROUPS = HEADS // TOGETHER
PIECES = 3
LOG2E = 1.4426950408889634
NN = (((1,), (0,)), ((), ()))
NT = (((1,), (1,)), ((), ()))
TN = (((0,), (0,)), ((), ()))
MESH = pl.DeviceIdType.MESH


def dot(a, b, dims=NN):
    return lax.dot_general(a, b, dims, preferred_element_type=jnp.float32)


def bit_of(index, bit):
    return (index // (1 << bit)) % 2


def aligned(start, size):
    return pl.ds(pl.multiple_of(start, size), size)


def fused_kernel(
    norm,
    x_hbm,
    w_hbm,
    g_hbm,
    gw_ref,
    gi_hbm,
    w,
    fr,
    gr,
    qkv,
    d,
    sums,
    back_out,
    back_in,
    ret,
    mine,
    held,
    landed,
    load_sem,
    x_send,
    x_recv,
    g_send,
    g_recv,
    halo_send,
    halo_recv,
    back_send,
    back_recv,
    ret_send,
    ret_recv,
    store_sem,
    rs_send,
    rs_recv,
):
    _, rows, width = x_hbm.shape
    head = width // HEADS
    cols = TOGETHER * head
    wide = 3 * cols
    scale = head ** (-0.5)
    streams, blocks = lax.axis_size("stream"), lax.axis_size("tm")
    stream, block = lax.axis_index("stream"), lax.axis_index("tm")
    side, place, places = block % 2, block // 2, blocks // 2
    other = 1 - side
    has_before, has_after = place > 0, place < places - 1
    stream_bits, block_bits = streams.bit_length() - 1, blocks.bit_length() - 1

    dims = [("stream", b, bit_of(stream, b)) for b in reversed(range(stream_bits))]
    dims += [("tm", b, bit_of(block, b)) for b in reversed(range(block_bits))]
    count = len(dims)
    core = stream_bits - 1
    far = list(reversed(range(core)))
    pair = count - 1
    along = list(reversed(range(stream_bits, count - 1)))
    order_a = [core] + far + along + [pair]
    order_c = [core, pair] + far + along
    order_d = [core] + along[:1] + far + along[1:] + [pair]
    orders = [[order_a, order_c, order_d]] * GROUPS

    def partner(k):
        axis, b, value = dims[k]
        return {axis: (stream if axis == "stream" else block) + (1 - 2 * value) * (1 << b)}

    beside = {"tm": block + 1 - 2 * side}
    after, before = {"tm": block + 2}, {"tm": block - 2}

    def remote(src, dst, send, recv, to):
        return pltpu.make_async_remote_copy(
            src_ref=src, dst_ref=dst, send_sem=send, recv_sem=recv, device_id=to, device_id_type=MESH
        )

    loads = []

    def load(src, dst):
        c = pltpu.make_async_copy(src, dst, load_sem.at[len(loads)])
        c.start()
        loads.append(c)
        return c

    piece = rows // PIECES

    def x_copy(i):
        return remote(
            x_hbm.at[other, pl.ds(i * piece, piece)],
            fr.at[aligned((1 + side) * rows + i * piece, piece)],
            x_send.at[i],
            x_recv.at[i],
            beside,
        )

    def g_copy(g):
        span = pl.ds(g * cols, cols)
        return remote(g_hbm.at[other, :, span], gr.at[side, :, span], g_send.at[g], g_recv.at[g], beside)

    def halo_copy(i):
        return remote(
            fr.at[pl.ds(2 * rows + i * piece, piece)],
            fr.at[pl.ds(i * piece, piece)],
            halo_send.at[i],
            halo_recv.at[i],
            after,
        )

    def back_copy(j):
        return remote(back_out.at[j], back_in.at[j], back_send.at[j], back_recv.at[j], before)

    def ret_copy(j):
        span = pl.ds(j * cols, cols)
        return remote(ret.at[j], gi_hbm.at[side, :, span], ret_send.at[j], ret_recv.at[j], beside)

    def project(slot, own_q):
        into = aligned(slot * rows, rows)

        def body(g, carry):
            if own_q:
                span = aligned(g * wide, wide)
            else:
                span = pl.ds(pl.multiple_of(g * wide + cols, cols), 2 * cols)
            qkv[into, span] = dot(fr[into, :], w[:, span]).astype(qkv.dtype)
            return carry

        lax.fori_loop(0, GROUPS, body, 0)

    def attend(b, g):
        keys = pl.ds(pl.multiple_of(b * rows, rows), 2 * rows)
        queries = aligned((b + 1) * rows, rows)
        bias = jnp.where(b + place > 0, 0.0, -1e30).astype(jnp.float32)
        factor = scale * LOG2E
        for t in range(TOGETHER):
            at = g * wide + t * head
            q = qkv[queries, at : at + head]
            k = qkv[keys, at + cols : at + cols + head]
            v = qkv[keys, at + 2 * cols : at + 2 * cols + head]
            go = gr[b, :, g * cols + t * head : g * cols + (t + 1) * head]
            s = dot(q, k, NT)
            s_prev, s_own = s[:, :rows], s[:, rows:]
            peak = jnp.maximum(
                jnp.max(s_own, 1, keepdims=True), jnp.max(s_prev, 1, keepdims=True) + bias
            )
            shift = peak * factor
            e_prev = jnp.exp2(s_prev * factor - (shift - bias * factor))
            e_own = jnp.exp2(s_own * factor - shift)
            e = jnp.concatenate([e_prev, e_own], 1)
            inverse = 1.0 / jnp.sum(e, 1, keepdims=True)
            dp = dot(go, v, NT)
            delta = jnp.sum(e * dp, 1, keepdims=True) * inverse
            p = e * inverse
            ds = (p * (dp - delta)).astype(jnp.bfloat16)
            pb = p.astype(jnp.bfloat16)
            d[queries, at : at + head] = (dot(ds, k) * scale).astype(d.dtype)
            for section, terms in ((1, dot(ds, q, TN) * scale), (2, dot(pb, go, TN))):
                span = slice(at + section * cols, at + section * cols + head)
                d[keys, span] = (d[keys, span].astype(jnp.float32) + terms).astype(d.dtype)

    def products(g, parity):
        part = width // streams

        def body(j, carry):
            index = 2 * j + parity
            span = aligned(index * part, part)
            lead = [bit_of(index, b) for b in reversed(range(stream_bits))]
            total = dot(fr[:, span], d[:, g * wide : (g + 1) * wide], TN).astype(held.dtype)
            shape = held.shape[2 + stream_bits :]
            for c in range(3):
                held[(g, c, *lead)] = total[:, c * cols : (c + 1) * cols].reshape(shape)
            return carry

        lax.fori_loop(0, streams // 2, body, 0)

    def region(g, c, phase, kept):
        order = orders[g][c]
        index = [slice(None)] * count
        for k in order[:phase]:
            index[k] = dims[k][2]
        last = order[phase]
        index[last] = dims[last][2] if kept else 1 - dims[last][2]
        return (g, c, *index)

    def rs_copy(g, c, phase):
        return remote(
            held.at[region(g, c, phase, False)],
            landed.at[region(g, c, phase, True)],
            rs_send.at[g, c, phase],
            rs_recv.at[g, c, phase],
            partner(orders[g][c][phase]),
        )

    def reduce(g, phase):
        for c in range(3):
            rs_copy(g, c, phase).wait_recv()
            kept, arrived = region(g, c, phase, True), region(g, c, phase, False)
            total = held[kept].astype(jnp.float32) + landed[arrived].astype(jnp.float32)
            if phase + 1 < count:
                held[kept] = total.astype(held.dtype)
                rs_copy(g, c, phase + 1).start()
            else:
                start = c * width + g * cols
                gw_ref[:, start : start + cols] = total * norm

    def weigh(g):
        products(g, 1 - dims[core][2])
        for c in range(3):
            rs_copy(g, c, 0).start()
        products(g, dims[core][2])

    def send_back():
        for j in range(GROUPS):
            span = slice(j * cols, (j + 1) * cols)
            terms = 0.0
            for g in range(GROUPS):
                at = slice(g * wide + cols, (g + 1) * wide)
                terms += dot(d[:rows, at], w[span, at], NT)
            back_out[j] = terms.astype(back_out.dtype)
            pl.when(has_before)(back_copy(j).start)

    def input_terms(b, j):
        at = aligned((b + 1) * rows, rows)
        sums[j] = dot(d[at, :], w[j * cols : (j + 1) * cols, :], NT)

    def add_back(j):
        back_copy(j).wait_recv()
        sums[j] += back_in[j].astype(jnp.float32)

    for g in range(GROUPS):
        for c in range(3):
            load(
                w_hbm.at[:, pl.ds(c * width + g * cols, cols)],
                w.at[:, pl.ds(g * wide + c * cols, cols)],
            )
    x_load = load(x_hbm.at[side], fr.at[aligned((1 + side) * rows, rows)])
    g_load = load(g_hbm.at[side], gr.at[side])
    barrier = pltpu.get_barrier_semaphore()

    def greet(to):
        pl.semaphore_signal(barrier, inc=1, device_id=to, device_id_type=MESH)

    for k in range(count):
        greet(partner(k))
    pl.when(has_before)(lambda: greet(before))
    pl.when(has_after)(lambda: greet(after))
    near = (place + places - 1) // places + (2 * places - 2 - place) // places
    pl.semaphore_wait(barrier, count + near)

    for i in range(PIECES):
        x_copy(i).start()
    d[...] = jnp.zeros_like(d)

    @pl.when(jnp.logical_not(has_before))
    def _():
        fr[:rows] = jnp.zeros((rows, width), fr.dtype)

    x_load.wait()

    @pl.when(jnp.logical_and(side == 1, has_after))
    def _():
        for i in range(PIECES):
            halo_copy(i).start()

    for c in loads[: 3 * GROUPS]:
        c.wait()
    project(1 + side, True)
    for i in range(PIECES):
        x_copy(i).wait_recv()
        pl.when(jnp.logical_and(side == 0, has_after))(halo_copy(i).start)
    for g in range(GROUPS):
        g_copy(g).start()
    project(1 + other, True)

    @pl.when(has_before)
    def _():
        for i in range(PIECES):
            halo_copy(i).wait_recv()

    project(0, False)
    g_load.wait()

    def own(g):
        attend(side, g)

    def moved(g):
        g_copy(g).wait_recv()
        attend(other, g)

    own(0)
    moved(0)
    weigh(0)
    own(1)
    reduce(0, 0)
    moved(1)
    weigh(1)
    reduce(0, 1)
    own(2)
    reduce(1, 0)
    own(3)
    pl.when(side == 0)(send_back)
    reduce(0, 2)
    reduce(1, 1)
    moved(2)
    weigh(2)
    reduce(0, 3)
    reduce(1, 2)
    moved(3)
    weigh(3)
    reduce(2, 0)
    pl.when(side == 1)(send_back)
    reduce(3, 0)

    for j in range(GROUPS):
        input_terms(other, j)
        pl.when(jnp.logical_and(side == 0, has_after))(functools.partial(add_back, j))
        ret[j] = sums[j].astype(ret.dtype)
        ret_copy(j).start()
    reduce(2, 1)
    reduce(3, 1)
    for j in range(GROUPS):
        input_terms(side, j)
    for phase in range(2, count):
        for g in range(GROUPS):
            if phase >= (4, 3, 2, 2)[g]:
                reduce(g, phase)

    stores = []
    for j in range(GROUPS):
        pl.when(jnp.logical_and(side == 1, has_after))(functools.partial(add_back, j))
        mine[j] = sums[j].astype(mine.dtype)
        span = pl.ds(j * cols, cols)
        store = pltpu.make_async_copy(mine.at[j], gi_hbm.at[side, :, span], store_sem.at[j])
        store.start()
        stores.append(store)

    for i in range(PIECES):
        x_copy(i).wait_send()
    for g in range(GROUPS):
        g_copy(g).wait_send()
        for c in range(3):
            for phase in range(count):
                rs_copy(g, c, phase).wait_send()

    @pl.when(has_after)
    def _():
        for i in range(PIECES):
            halo_copy(i).wait_send()

    @pl.when(has_before)
    def _():
        for j in range(GROUPS):
            back_copy(j).wait_send()

    for j in range(GROUPS):
        ret_copy(j).wait_send()
        ret_copy(j).wait_recv()
        stores[j].wait()


def local(x, w_qkv, g):
    records, rows, width = x.shape
    streams, blocks = lax.axis_size("stream"), lax.axis_size("tm")
    devices = streams * blocks
    count = devices.bit_length() - 1
    cols = width // GROUPS
    total_frames = records * rows * devices
    part = pltpu.VMEM((GROUPS, 3, *([2] * count), width // devices, cols), jnp.bfloat16)
    tiles = pltpu.VMEM((GROUPS, rows, cols), jnp.bfloat16)
    dma = lambda *shape: pltpu.SemaphoreType.DMA(shape)
    half = lambda *shape: pltpu.VMEM(shape, jnp.bfloat16)
    grad_w, grad_in = pl.pallas_call(
        functools.partial(fused_kernel, float(total_frames) ** (-0.5)),
        in_specs=[pl.BlockSpec(memory_space=pl.ANY)] * 3,
        out_specs=[pl.BlockSpec(memory_space=pltpu.VMEM), pl.BlockSpec(memory_space=pl.ANY)],
        out_shape=(
            jax.ShapeDtypeStruct((width // devices, 3 * width), jnp.float32),
            jax.ShapeDtypeStruct((records, rows, width), jnp.bfloat16),
        ),
        scratch_shapes=[
            half(width, 3 * width),
            half(3 * rows, width),
            half(2, rows, width),
            half(3 * rows, 3 * width),
            half(3 * rows, 3 * width),
            pltpu.VMEM((GROUPS, rows, cols), jnp.float32),
            tiles,
            tiles,
            tiles,
            tiles,
            part,
            part,
            dma(3 * GROUPS + 2),
            dma(PIECES),
            dma(PIECES),
            dma(GROUPS),
            dma(GROUPS),
            dma(PIECES),
            dma(PIECES),
            dma(GROUPS),
            dma(GROUPS),
            dma(GROUPS),
            dma(GROUPS),
            dma(GROUPS),
            dma(GROUPS, 3, count),
            dma(GROUPS, 3, count),
        ],
        compiler_params=pltpu.CompilerParams(
            collective_id=0, has_side_effects=True, vmem_limit_bytes=60 << 20
        ),
        cost_estimate=pl.CostEstimate(
            flops=32 * records * rows * width * width,
            bytes_accessed=6 * w_qkv.size,
            transcendentals=4 * HEADS * rows * rows,
        ),
    )(x, w_qkv, g)
    return grad_in, grad_w


def solution(mesh):
    return jax.shard_map(
        local,
        mesh=mesh,
        in_specs=(P("stream", "tm", None), P(), P("stream", "tm", None)),
        out_specs=(P("stream", "tm", None), P(("stream", "tm"), None)),
        check_vma=False,
    )
```

```python
import functools

import jax
import jax.numpy as jnp
from jax import lax
from jax.experimental import pallas as pl
from jax.experimental.pallas import tpu as pltpu
from jax.sharding import PartitionSpec as P

HEADS = 8
TOGETHER = 2
GROUPS = HEADS // TOGETHER
PIECES = 6
EARLY = 4
LOG2E = 1.4426950408889634
NN = (((1,), (0,)), ((), ()))
NT = (((1,), (1,)), ((), ()))
TN = (((0,), (0,)), ((), ()))
MESH = pl.DeviceIdType.MESH


def dot(a, b, dims=NN):
    return lax.dot_general(a, b, dims, preferred_element_type=jnp.float32)


def bit_of(index, bit):
    return (index // (1 << bit)) % 2


def aligned(start, size):
    return pl.ds(pl.multiple_of(start, size), size)


def fused_kernel(
    norm,
    x_hbm,
    w_hbm,
    g_hbm,
    gw_ref,
    gi_hbm,
    w,
    fr,
    gr,
    qkv,
    d,
    sums,
    back_out,
    back_in,
    ret,
    mine,
    held,
    landed,
    load_sem,
    x_send,
    x_recv,
    g_send,
    g_recv,
    halo_send,
    halo_recv,
    back_send,
    back_recv,
    ret_send,
    ret_recv,
    store_sem,
    rs_send,
    rs_recv,
):
    _, rows, width = x_hbm.shape
    head = width // HEADS
    cols = TOGETHER * head
    pairs = 2 * cols
    scale = head ** (-0.5)
    streams, blocks = lax.axis_size("stream"), lax.axis_size("tm")
    stream, block = lax.axis_index("stream"), lax.axis_index("tm")
    side, place, places = block % 2, block // 2, blocks // 2
    other = 1 - side
    has_before, has_after = place > 0, place < places - 1
    stream_bits, block_bits = streams.bit_length() - 1, blocks.bit_length() - 1

    dims = [("stream", b, bit_of(stream, b)) for b in reversed(range(stream_bits))]
    dims += [("tm", b, bit_of(block, b)) for b in reversed(range(block_bits))]
    count = len(dims)
    core = stream_bits - 1
    far = list(reversed(range(core)))
    pair = count - 1
    along = list(reversed(range(stream_bits, count - 1)))
    order_a = [core] + far + along + [pair]
    order_c = [core, pair] + far + along
    order_e = [core] + far + [pair] + along
    orders = [
        [order_e, order_e, order_c],
        [order_e, order_c, order_e],
        [order_e, order_e, order_e],
        [order_a, order_a, order_a],
    ]

    def partner(k):
        axis, b, value = dims[k]
        return {axis: (stream if axis == "stream" else block) + (1 - 2 * value) * (1 << b)}

    beside = {"tm": block + 1 - 2 * side}
    after, before = {"tm": block + 2}, {"tm": block - 2}

    def remote(src, dst, send, recv, to):
        return pltpu.make_async_remote_copy(
            src_ref=src, dst_ref=dst, send_sem=send, recv_sem=recv, device_id=to, device_id_type=MESH
        )

    loads = []

    def load(src, dst):
        c = pltpu.make_async_copy(src, dst, load_sem.at[len(loads)])
        c.start()
        loads.append(c)
        return c

    piece = rows // PIECES

    def x_copy(i):
        return remote(
            x_hbm.at[other, pl.ds(i * piece, piece)],
            fr.at[aligned((1 + side) * rows + i * piece, piece)],
            x_send.at[i],
            x_recv.at[i],
            beside,
        )

    def g_copy(g):
        span = pl.ds(g * cols, cols)
        return remote(g_hbm.at[other, :, span], gr.at[side, :, span], g_send.at[g], g_recv.at[g], beside)

    def halo_copy(i):
        return remote(
            fr.at[pl.ds(2 * rows + i * piece, piece)],
            fr.at[pl.ds(i * piece, piece)],
            halo_send.at[i],
            halo_recv.at[i],
            after,
        )

    def back_copy(j):
        return remote(back_out.at[j], back_in.at[j], back_send.at[j], back_recv.at[j], before)

    def ret_copy(j):
        span = pl.ds(j * cols, cols)
        return remote(ret.at[j], gi_hbm.at[side, :, span], ret_send.at[j], ret_recv.at[j], beside)

    def project(slot, start, low=0, high=PIECES):
        into = pl.ds(pl.multiple_of(slot * rows + low * piece, piece), (high - low) * piece)

        def body(j, carry):
            span = aligned(start + j * width, width)
            qkv[into, span] = dot(fr[into, :], w[:, span]).astype(qkv.dtype)
            return carry

        lax.fori_loop(0, (3 * width - start) // width, body, 0)

    def attend(b, g):
        keys = pl.ds(pl.multiple_of(b * rows, rows), 2 * rows)
        queries = aligned((b + 1) * rows, rows)
        bias = jnp.where(b + place > 0, 0.0, -1e30).astype(jnp.float32)
        factor = scale * LOG2E
        def at(start):
            return pl.ds(pl.multiple_of(start, head), head)

        for t in range(TOGETHER):
            for_q = at(g * cols + t * head)
            for_k = at(width + g * pairs + t * head)
            for_v = at(width + g * pairs + cols + t * head)
            q, k, v, go = qkv[queries, for_q], qkv[keys, for_k], qkv[keys, for_v], gr[b, :, for_q]
            s = dot(q, k, NT)
            s_prev, s_own = s[:, :rows], s[:, rows:]
            peak = jnp.maximum(
                jnp.max(s_own, 1, keepdims=True), jnp.max(s_prev, 1, keepdims=True) + bias
            )
            shift = peak * factor
            e_prev = jnp.exp2(s_prev * factor - (shift - bias * factor))
            e_own = jnp.exp2(s_own * factor - shift)
            e = jnp.concatenate([e_prev, e_own], 1)
            inverse = 1.0 / jnp.sum(e, 1, keepdims=True)
            dp = dot(go, v, NT)
            delta = jnp.sum(e * dp, 1, keepdims=True) * inverse
            p = e * inverse
            ds = (p * (dp - delta)).astype(jnp.bfloat16)
            pb = p.astype(jnp.bfloat16)
            d[queries, for_q] = (dot(ds, k) * scale).astype(d.dtype)
            for span, terms in ((for_k, dot(ds, q, TN) * scale), (for_v, dot(pb, go, TN))):
                d[keys, span] = (d[keys, span].astype(jnp.float32) + terms).astype(d.dtype)

    def region(g, c, phase, kept):
        order = orders[g][c] if phase else [core]
        index = [slice(None)] * count
        for k in order[:phase]:
            index[k] = dims[k][2]
        last = order[phase]
        index[last] = dims[last][2] if kept else 1 - dims[last][2]
        return (g, c, *index)

    def rs_copy(g, c, phase):
        return remote(
            held.at[region(g, c, phase, False)],
            landed.at[region(g, c, phase, True)],
            rs_send.at[g, c, phase],
            rs_recv.at[g, c, phase],
            partner(orders[g][c][phase] if phase else core),
        )

    def reduce(g, c, phase):
        rs_copy(g, c, phase).wait_recv()
        kept, arrived = region(g, c, phase, True), region(g, c, phase, False)
        total = held[kept].astype(jnp.float32) + landed[arrived].astype(jnp.float32)
        if phase + 1 < count:
            held[kept] = total.astype(held.dtype)
            rs_copy(g, c, phase + 1).start()
        else:
            start = c * width + g * cols
            gw_ref[:, start : start + cols] = total * norm

    def weigh(g):
        shape = held.shape[2:]
        at = pl.ds(pl.multiple_of(width + g * pairs, pairs), pairs)
        total = dot(fr[...], d[:, at], TN).astype(held.dtype)
        for c in (1, 2):
            held[g, c] = total[:, (c - 1) * cols : c * cols].reshape(shape)
            rs_copy(g, c, 0).start()
        total = dot(fr[rows:, :], d[rows:, aligned(g * cols, cols)], TN).astype(held.dtype)
        held[g, 0] = total.reshape(shape)
        rs_copy(g, 0, 0).start()

    def back_terms():
        half = 2 * cols

        def body(i, carry):
            terms = dot(d[:rows, width:], w[aligned(i * half, half), width:], NT).astype(back_out.dtype)
            for j in range(2):
                back_out[2 * i + j] = terms[:, j * cols : (j + 1) * cols]
            return carry

        lax.fori_loop(0, GROUPS // 2, body, 0)

    def send_back(j):
        pl.when(has_before)(back_copy(j).start)

    def input_terms(b, into):
        at = aligned((b + 1) * rows, rows)

        half = 2 * cols

        def body(i, carry):
            terms = dot(d[at, :], w[aligned(i * half, half), :], NT)
            for j in range(2):
                sums[into, 2 * i + j] = terms[:, j * cols : (j + 1) * cols]
            return carry

        lax.fori_loop(0, GROUPS // 2, body, 0)

    def add_back(into, j):
        back_copy(j).wait_recv()
        sums[into, j] += back_in[j].astype(jnp.float32)

    def store(j):
        span = pl.ds(j * cols, cols)
        return pltpu.make_async_copy(mine.at[j], gi_hbm.at[side, :, span], store_sem.at[j])

    for g in range(GROUPS):
        for c in range(3):
            load(
                w_hbm.at[:, pl.ds(c * width + g * cols, cols)],
                w.at[:, pl.ds(g * cols if c == 0 else width + g * pairs + (c - 1) * cols, cols)],
            )
    x_load = load(x_hbm.at[side], fr.at[aligned((1 + side) * rows, rows)])
    g_load = load(g_hbm.at[side], gr.at[side])
    barrier = pltpu.get_barrier_semaphore()

    def greet(to):
        pl.semaphore_signal(barrier, inc=1, device_id=to, device_id_type=MESH)

    for k in range(count):
        greet(partner(k))
    pl.when(has_before)(lambda: greet(before))
    pl.when(has_after)(lambda: greet(after))
    near = (place + places - 1) // places + (2 * places - 2 - place) // places
    pl.semaphore_wait(barrier, count + near)

    for i in range(PIECES):
        x_copy(i).start()
    for g in range(GROUPS):
        g_copy(g).start()
    d[...] = jnp.zeros_like(d)

    @pl.when(jnp.logical_not(has_before))
    def _():
        fr[:rows] = jnp.zeros((rows, width), fr.dtype)

    x_load.wait()

    @pl.when(jnp.logical_and(side == 1, has_after))
    def _():
        for i in range(PIECES):
            halo_copy(i).start()

    for c in loads[: 3 * GROUPS]:
        c.wait()
    project(1 + side, 0)
    for i in range(PIECES):
        x_copy(i).wait_recv()
        pl.when(jnp.logical_and(side == 0, has_after))(halo_copy(i).start)
        if i == EARLY - 1:
            project(1 + other, 0, 0, EARLY)
    project(1 + other, 0, EARLY, PIECES)
    g_load.wait()

    def meet(g):
        g_copy(g).wait_recv()

    def halo():
        @pl.when(has_before)
        def _():
            for i in range(PIECES):
                halo_copy(i).wait_recv()

        project(0, width)

    def give(j):
        ret[j] = sums[0, j].astype(ret.dtype)
        ret_copy(j).start()

    def give_soon():
        for j in range(GROUPS):
            give(j)

    def give_late(j):
        @pl.when(side == 0)
        def _():
            pl.when(has_after)(functools.partial(add_back, 0, j))
            give(j)

    def keep(j):
        pl.when(jnp.logical_and(side == 1, has_after))(functools.partial(add_back, 1, j))
        mine[j] = sums[1, j].astype(mine.dtype)
        store(j).start()

    def reduce_all(g, phase):
        for c in range(3):
            reduce(g, c, phase)

    turns = ((1, 0), (0, 0), (0, 1), (1, 1), (0, 2), (0, 3), (1, 2), (1, 3))
    block_table = sum(b << i for i, (b, _) in enumerate(turns))
    group_table = sum(g << (2 * i) for i, (_, g) in enumerate(turns))

    def turn(i, carry):
        b = (block_table >> i) % 2
        g = (group_table >> (2 * i)) % GROUPS

        @pl.when(i == 0)
        def _():
            pl.when(side == 0)(functools.partial(meet, 0))

        for at, arriving in ((2, 1), (4, 2), (5, 3)):
            pl.when(i == at)(functools.partial(meet, arriving))
        attend(b, g)

        @pl.when(i == 0)
        def _():
            halo()
            pl.when(side == 1)(functools.partial(meet, 0))

        @pl.when(i == 4)
        def _():
            reduce_all(0, 1)

        @pl.when(i == 5)
        def _():
            back_terms()
            send_back(0)
            send_back(1)
            reduce_all(1, 1)

        @pl.when(i == 6)
        def _():
            reduce_all(0, 2)

        @pl.when(jnp.logical_or(i == 1, jnp.logical_or(i == 3, i == 6)))
        def _():
            weigh(g)

        for at, group in ((1, 0), (3, 1), (6, 2)):
            pl.when(i == at)(functools.partial(reduce_all, group, 0))
        return carry

    lax.fori_loop(0, len(turns), turn, 0)
    done = [[3] * 3, [2] * 3, [1] * 3, [0] * 3]

    def step(g, ready=(0, 1, 2)):
        for c in ready:
            if done[g][c] < count:
                reduce(g, c, done[g][c])
                done[g][c] += 1

    def slant(g):
        ahead = [True, done[g][0] - done[g][1] >= 1, done[g][1] - done[g][2] >= 1]
        full = [n >= count - 1 for n in done[g]]
        ready = [c for c in range(3) if ahead[c] or (c and full[c - 1])]
        step(g, [c for c in ready if not full[c]])

    step(1)
    send_back(2)
    send_back(3)
    input_terms(other, 0)
    pl.when(side == 1)(functools.partial(give, 0))
    give_late(0)
    weigh(3)
    step(3)
    pl.when(side == 1)(functools.partial(give, 1))
    give_late(1)
    step(2)
    step(0)
    input_terms(side, 1)
    pl.when(side == 1)(functools.partial(give, 2))
    give_late(2)
    step(1)
    slant(3)
    pl.when(side == 1)(functools.partial(give, 3))
    give_late(3)
    slant(3)
    slant(3)
    step(2)
    slant(3)
    step(0)
    step(1)
    step(2)
    slant(3)
    for j in range(GROUPS):
        keep(j)
    for _ in range(count):
        for g in range(GROUPS):
            slant(g)
    for g in range(GROUPS):
        step(g)

    for i in range(PIECES):
        x_copy(i).wait_send()
    for g in range(GROUPS):
        g_copy(g).wait_send()
        for c in range(3):
            for phase in range(count):
                rs_copy(g, c, phase).wait_send()

    @pl.when(has_after)
    def _():
        for i in range(PIECES):
            halo_copy(i).wait_send()

    @pl.when(has_before)
    def _():
        for j in range(GROUPS):
            back_copy(j).wait_send()

    for j in range(GROUPS):
        ret_copy(j).wait_send()
        ret_copy(j).wait_recv()
        store(j).wait()


def leave_kernel(a_hbm, b_hbm, a_out, b_out, a_held, b_held, sems):
    parts = [(b_hbm, b_held, b_out)]
    step = a_hbm.shape[1] // 2
    for r in range(a_hbm.shape[0]):
        for i in range(2):
            at = (r, pl.ds(i * step, step))
            parts.append((a_hbm.at[at], a_held.at[at], a_out.at[at]))
    first = [pltpu.make_async_copy(p[0], p[1], sems.at[0, i]) for i, p in enumerate(parts)]
    second = [pltpu.make_async_copy(p[1], p[2], sems.at[1, i]) for i, p in enumerate(parts)]
    for c in first:
        c.start()
    for c, then in zip(first, second):
        c.wait()
        then.start()
    for c in second:
        c.wait()


def leave(a, b):
    return pl.pallas_call(
        leave_kernel,
        in_specs=[pl.BlockSpec(memory_space=pl.ANY)] * 2,
        out_specs=[pl.BlockSpec(memory_space=pl.ANY)] * 2,
        out_shape=[jax.ShapeDtypeStruct(t.shape, t.dtype) for t in (a, b)],
        scratch_shapes=[pltpu.VMEM(t.shape, t.dtype) for t in (a, b)]
        + [pltpu.SemaphoreType.DMA((2, 1 + 2 * a.shape[0]))],
    )(a, b)


def local(x, w_qkv, g):
    records, rows, width = x.shape
    streams, blocks = lax.axis_size("stream"), lax.axis_size("tm")
    devices = streams * blocks
    count = devices.bit_length() - 1
    cols = width // GROUPS
    total_frames = records * rows * devices
    part = pltpu.VMEM((GROUPS, 3, *([2] * count), width // devices, cols), jnp.bfloat16)
    tiles = pltpu.VMEM((GROUPS, rows, cols), jnp.bfloat16)
    dma = lambda *shape: pltpu.SemaphoreType.DMA(shape)
    half = lambda *shape: pltpu.VMEM(shape, jnp.bfloat16)
    grad_w, grad_in = pl.pallas_call(
        functools.partial(fused_kernel, float(total_frames) ** (-0.5)),
        in_specs=[pl.BlockSpec(memory_space=pl.ANY)] * 3,
        out_specs=[pl.BlockSpec(memory_space=pltpu.VMEM), pl.BlockSpec(memory_space=pl.ANY)],
        out_shape=(
            jax.ShapeDtypeStruct((width // devices, 3 * width), jnp.float32),
            jax.ShapeDtypeStruct((records, rows, width), jnp.bfloat16),
        ),
        scratch_shapes=[
            half(width, 3 * width),
            half(3 * rows, width),
            half(2, rows, width),
            half(3 * rows, 3 * width),
            half(3 * rows, 3 * width),
            pltpu.VMEM((2, GROUPS, rows, cols), jnp.float32),
            tiles,
            tiles,
            tiles,
            tiles,
            part,
            part,
            dma(3 * GROUPS + 2),
            dma(PIECES),
            dma(PIECES),
            dma(GROUPS),
            dma(GROUPS),
            dma(PIECES),
            dma(PIECES),
            dma(GROUPS),
            dma(GROUPS),
            dma(GROUPS),
            dma(GROUPS),
            dma(GROUPS),
            dma(GROUPS, 3, count),
            dma(GROUPS, 3, count),
        ],
        compiler_params=pltpu.CompilerParams(
            collective_id=0, has_side_effects=True, vmem_limit_bytes=60 << 20
        ),
        cost_estimate=pl.CostEstimate(
            flops=32 * records * rows * width * width,
            bytes_accessed=6 * w_qkv.size,
            transcendentals=4 * HEADS * rows * rows,
        ),
    )(x, w_qkv, g)
    return tuple(leave(grad_in, grad_w))


def solution(mesh):
    return jax.shard_map(
        local,
        mesh=mesh,
        in_specs=(P("stream", "tm", None), P(), P("stream", "tm", None)),
        out_specs=(P("stream", "tm", None), P(("stream", "tm"), None)),
        check_vma=False,
    )
```

```python
import functools

import jax
import jax.numpy as jnp
from jax import lax
from jax.experimental import pallas as pl
from jax.experimental.pallas import tpu as pltpu
from jax.sharding import PartitionSpec as P

HEADS = 8
TOGETHER = 2
GROUPS = HEADS // TOGETHER
PIECES = 6
EARLY = 4
LOG2E = 1.4426950408889634
NN = (((1,), (0,)), ((), ()))
NT = (((1,), (1,)), ((), ()))
TN = (((0,), (0,)), ((), ()))
MESH = pl.DeviceIdType.MESH


def dot(a, b, dims=NN):
    return lax.dot_general(a, b, dims, preferred_element_type=jnp.float32)


def bit_of(index, bit):
    return (index // (1 << bit)) % 2


def aligned(start, size):
    return pl.ds(pl.multiple_of(start, size), size)


def fused_kernel(
    norm,
    x_hbm,
    w_hbm,
    g_hbm,
    gw_hbm,
    gi_hbm,
    w,
    fr,
    gr,
    qkv,
    d,
    sums,
    back_out,
    back_in,
    ret,
    mine,
    gw,
    held,
    landed,
    load_sem,
    x_send,
    x_recv,
    g_send,
    g_recv,
    halo_send,
    halo_recv,
    back_send,
    back_recv,
    ret_send,
    ret_recv,
    store_sem,
    rs_send,
    rs_recv,
):
    _, rows, width = x_hbm.shape
    head = width // HEADS
    cols = TOGETHER * head
    pairs = 2 * cols
    scale = head ** (-0.5)
    streams, blocks = lax.axis_size("stream"), lax.axis_size("tm")
    stream, block = lax.axis_index("stream"), lax.axis_index("tm")
    side, place, places = block % 2, block // 2, blocks // 2
    other = 1 - side
    has_before, has_after = place > 0, place < places - 1
    stream_bits, block_bits = streams.bit_length() - 1, blocks.bit_length() - 1

    dims = [("stream", b, bit_of(stream, b)) for b in reversed(range(stream_bits))]
    dims += [("tm", b, bit_of(block, b)) for b in reversed(range(block_bits))]
    count = len(dims)
    core = stream_bits - 1
    far = list(reversed(range(core)))
    pair = count - 1
    along = list(reversed(range(stream_bits, count - 1)))
    order_a = [core] + far + along + [pair]
    order_c = [core, pair] + far + along
    order_e = [core] + far + [pair] + along
    orders = [
        [order_e, order_e, order_c],
        [order_e, order_c, order_e],
        [order_c, order_e, order_c],
        [order_a, order_c, order_a],
    ]

    def partner(k):
        axis, b, value = dims[k]
        return {axis: (stream if axis == "stream" else block) + (1 - 2 * value) * (1 << b)}

    beside = {"tm": block + 1 - 2 * side}
    after, before = {"tm": block + 2}, {"tm": block - 2}

    def remote(src, dst, send, recv, to):
        return pltpu.make_async_remote_copy(
            src_ref=src, dst_ref=dst, send_sem=send, recv_sem=recv, device_id=to, device_id_type=MESH
        )

    loads = []

    def load(src, dst):
        c = pltpu.make_async_copy(src, dst, load_sem.at[len(loads)])
        c.start()
        loads.append(c)
        return c

    piece = rows // PIECES

    def x_copy(i):
        return remote(
            x_hbm.at[other, pl.ds(i * piece, piece)],
            fr.at[aligned((1 + side) * rows + i * piece, piece)],
            x_send.at[i],
            x_recv.at[i],
            beside,
        )

    def g_copy(g):
        span = pl.ds(g * cols, cols)
        return remote(g_hbm.at[other, :, span], gr.at[side, :, span], g_send.at[g], g_recv.at[g], beside)

    def halo_copy(i):
        return remote(
            fr.at[pl.ds(2 * rows + i * piece, piece)],
            fr.at[pl.ds(i * piece, piece)],
            halo_send.at[i],
            halo_recv.at[i],
            after,
        )

    def back_copy(j):
        return remote(back_out.at[j], back_in.at[j], back_send.at[j], back_recv.at[j], before)

    def ret_copy(j):
        span = pl.ds(j * cols, cols)
        return remote(ret.at[j], gi_hbm.at[side, :, span], ret_send.at[j], ret_recv.at[j], beside)

    def project(slot, start, low=0, high=PIECES):
        into = pl.ds(pl.multiple_of(slot * rows + low * piece, piece), (high - low) * piece)

        def body(j, carry):
            span = aligned(start + j * width, width)
            qkv[into, span] = dot(fr[into, :], w[:, span]).astype(qkv.dtype)
            return carry

        lax.fori_loop(0, (3 * width - start) // width, body, 0)

    def attend(b, g):
        keys = pl.ds(pl.multiple_of(b * rows, rows), 2 * rows)
        queries = aligned((b + 1) * rows, rows)
        bias = jnp.where(b + place > 0, 0.0, -1e30).astype(jnp.float32)
        factor = scale * LOG2E
        def at(start):
            return pl.ds(pl.multiple_of(start, head), head)

        for t in range(TOGETHER):
            for_q = at(g * cols + t * head)
            for_k = at(width + g * pairs + t * head)
            for_v = at(width + g * pairs + cols + t * head)
            q, k, v, go = qkv[queries, for_q], qkv[keys, for_k], qkv[keys, for_v], gr[b, :, for_q]
            s = dot(q, k, NT)
            s_prev, s_own = s[:, :rows], s[:, rows:]
            peak = jnp.maximum(
                jnp.max(s_own, 1, keepdims=True), jnp.max(s_prev, 1, keepdims=True) + bias
            )
            shift = peak * factor
            e_prev = jnp.exp2(s_prev * factor - (shift - bias * factor))
            e_own = jnp.exp2(s_own * factor - shift)
            e = jnp.concatenate([e_prev, e_own], 1)
            inverse = 1.0 / jnp.sum(e, 1, keepdims=True)
            dp = dot(go, v, NT)
            delta = jnp.sum(e * dp, 1, keepdims=True) * inverse
            p = e * inverse
            ds = (p * (dp - delta)).astype(jnp.bfloat16)
            pb = p.astype(jnp.bfloat16)
            d[queries, for_q] = (dot(ds, k) * scale).astype(d.dtype)
            for span, terms in ((for_k, dot(ds, q, TN) * scale), (for_v, dot(pb, go, TN))):
                d[keys, span] = (d[keys, span].astype(jnp.float32) + terms).astype(d.dtype)

    def region(g, c, phase, kept):
        order = orders[g][c] if phase else [core]
        index = [slice(None)] * count
        for k in order[:phase]:
            index[k] = dims[k][2]
        last = order[phase]
        index[last] = dims[last][2] if kept else 1 - dims[last][2]
        return (g, c, *index)

    def rs_copy(g, c, phase):
        return remote(
            held.at[region(g, c, phase, False)],
            landed.at[region(g, c, phase, True)],
            rs_send.at[g, c],
            rs_recv.at[g, c, phase],
            partner(orders[g][c][phase] if phase else core),
        )

    def reduce(g, c, phase):
        rs_copy(g, c, phase).wait_recv()
        kept, arrived = region(g, c, phase, True), region(g, c, phase, False)
        total = held[kept].astype(jnp.float32) + landed[arrived].astype(jnp.float32)
        if phase + 1 < count:
            held[kept] = total.astype(held.dtype)
            rs_copy(g, c, phase).wait_send()
            rs_copy(g, c, phase + 1).start()
        else:
            start = c * width + g * cols
            gw[:, start : start + cols] = total * norm

    def weigh(g):
        shape = held.shape[2:]
        at = pl.ds(pl.multiple_of(width + g * pairs, pairs), pairs)
        total = dot(fr[...], d[:, at], TN).astype(held.dtype)
        for c in (1, 2):
            held[g, c] = total[:, (c - 1) * cols : c * cols].reshape(shape)
            rs_copy(g, c, 0).start()
        total = dot(fr[rows:, :], d[rows:, aligned(g * cols, cols)], TN).astype(held.dtype)
        held[g, 0] = total.reshape(shape)
        rs_copy(g, 0, 0).start()

    def back_terms():
        half = 2 * cols

        def body(i, carry):
            terms = dot(d[:rows, width:], w[aligned(i * half, half), width:], NT).astype(back_out.dtype)
            for j in range(2):
                back_out[2 * i + j] = terms[:, j * cols : (j + 1) * cols]
            return carry

        lax.fori_loop(0, GROUPS // 2, body, 0)

    def send_back(j):
        pl.when(has_before)(back_copy(j).start)

    def input_terms(b, into):
        at = aligned((b + 1) * rows, rows)

        half = 2 * cols

        def body(i, carry):
            terms = dot(d[at, :], w[aligned(i * half, half), :], NT)
            for j in range(2):
                sums[into, 2 * i + j] = terms[:, j * cols : (j + 1) * cols]
            return carry

        lax.fori_loop(0, GROUPS // 2, body, 0)

    def add_back(into, j):
        back_copy(j).wait_recv()
        sums[into, j] += back_in[j].astype(jnp.float32)

    def store(j):
        span = pl.ds(j * cols, cols)
        return pltpu.make_async_copy(mine.at[j], gi_hbm.at[side, :, span], store_sem.at[j])

    for g in range(GROUPS):
        for c in range(3):
            load(
                w_hbm.at[:, pl.ds(c * width + g * cols, cols)],
                w.at[:, pl.ds(g * cols if c == 0 else width + g * pairs + (c - 1) * cols, cols)],
            )
    x_load = load(x_hbm.at[side], fr.at[aligned((1 + side) * rows, rows)])
    g_load = load(g_hbm.at[side], gr.at[side])
    barrier = pltpu.get_barrier_semaphore()

    def greet(to):
        pl.semaphore_signal(barrier, inc=1, device_id=to, device_id_type=MESH)

    for k in range(count):
        greet(partner(k))
    pl.when(has_before)(lambda: greet(before))
    pl.when(has_after)(lambda: greet(after))
    near = (place + places - 1) // places + (2 * places - 2 - place) // places
    pl.semaphore_wait(barrier, count + near)

    for i in range(PIECES):
        x_copy(i).start()
    for g in range(GROUPS):
        g_copy(g).start()
    d[...] = jnp.zeros_like(d)

    @pl.when(jnp.logical_not(has_before))
    def _():
        fr[:rows] = jnp.zeros((rows, width), fr.dtype)

    x_load.wait()

    @pl.when(jnp.logical_and(side == 1, has_after))
    def _():
        for i in range(PIECES):
            halo_copy(i).start()

    for c in loads[: 3 * GROUPS]:
        c.wait()
    project(1 + side, 0)
    for i in range(PIECES):
        x_copy(i).wait_recv()
        pl.when(jnp.logical_and(side == 0, has_after))(halo_copy(i).start)
        if i == EARLY - 1:
            project(1 + other, 0, 0, EARLY)
    project(1 + other, 0, EARLY, PIECES)
    g_load.wait()

    def meet(g):
        g_copy(g).wait_recv()

    def halo():
        @pl.when(has_before)
        def _():
            for i in range(PIECES):
                halo_copy(i).wait_recv()

        project(0, width)

    def give(j):
        ret[j] = sums[0, j].astype(ret.dtype)
        ret_copy(j).start()

    def give_soon():
        for j in range(GROUPS):
            give(j)

    def give_late(j):
        @pl.when(side == 0)
        def _():
            pl.when(has_after)(functools.partial(add_back, 0, j))
            give(j)

    def keep(j):
        pl.when(jnp.logical_and(side == 1, has_after))(functools.partial(add_back, 1, j))
        mine[j] = sums[1, j].astype(mine.dtype)
        store(j).start()

    def reduce_all(g, phase):
        for c in range(3):
            reduce(g, c, phase)

    turns = ((0, 0), (1, 0), (0, 1), (1, 1), (0, 2), (0, 3), (1, 2), (1, 3))
    block_table = sum(b << i for i, (b, _) in enumerate(turns))
    group_table = sum(g << (2 * i) for i, (_, g) in enumerate(turns))

    def turn(i, carry):
        b = ((block_table >> i) + side * ((3 >> i) % 2)) % 2
        g = (group_table >> (2 * i)) % GROUPS

        pl.when(jnp.logical_and(i == 0, side == 0))(halo)
        for at, arriving in ((1, 0), (2, 1), (4, 2), (5, 3)):
            pl.when(i == at)(functools.partial(meet, arriving))
        attend(b, g)

        pl.when(jnp.logical_and(i == 0, side == 1))(halo)

        @pl.when(i == 4)
        def _():
            reduce_all(0, 1)

        @pl.when(i == 5)
        def _():
            back_terms()
            send_back(0)
            send_back(1)
            reduce_all(1, 1)

        @pl.when(i == 6)
        def _():
            reduce_all(0, 2)
            send_back(2)
            send_back(3)

        @pl.when(jnp.logical_or(i == 1, jnp.logical_or(i == 3, i == 6)))
        def _():
            weigh(g)

        for at, group in ((1, 0), (3, 1), (6, 2)):
            pl.when(i == at)(functools.partial(reduce_all, group, 0))
        return carry

    lax.fori_loop(0, len(turns), turn, 0)
    done = [[3] * 3, [2] * 3, [1] * 3, [0] * 3]

    def step(g, ready=(0, 1, 2)):
        for c in ready:
            if done[g][c] < count:
                reduce(g, c, done[g][c])
                done[g][c] += 1

    def slant(g):
        ahead = [True, done[g][0] - done[g][1] >= 1, done[g][1] - done[g][2] >= 1]
        full = [n >= count - 1 for n in done[g]]
        ready = [c for c in (2, 1, 0) if ahead[c] or (c and full[c - 1])]
        step(g, [c for c in ready if not full[c]])

    step(1)
    input_terms(other, 0)
    pl.when(side == 1)(functools.partial(give, 0))
    give_late(0)
    pl.when(side == 1)(functools.partial(give, 1))
    weigh(3)
    step(3)
    give_late(1)
    step(2)
    step(0)
    input_terms(side, 1)
    pl.when(side == 1)(functools.partial(give, 2))
    give_late(2)
    slant(3)
    pl.when(side == 1)(functools.partial(give, 3))
    slant(3)
    give_late(3)
    step(1)
    slant(3)
    step(2)
    slant(3)
    step(2)
    slant(3)
    step(0)
    step(1)
    for j in range(GROUPS):
        keep(j)
    for _ in range(count):
        for g in range(GROUPS):
            slant(g)
    for g in range(GROUPS):
        step(g)

    gw_store = pltpu.make_async_copy(gw, gw_hbm, load_sem.at[0])
    gw_store.start()

    for i in range(PIECES):
        x_copy(i).wait_send()
    for g in range(GROUPS):
        g_copy(g).wait_send()
        for c in range(3):
            rs_copy(g, c, count - 1).wait_send()

    @pl.when(has_after)
    def _():
        for i in range(PIECES):
            halo_copy(i).wait_send()

    @pl.when(has_before)
    def _():
        for j in range(GROUPS):
            back_copy(j).wait_send()

    for j in range(GROUPS):
        ret_copy(j).wait_send()
        ret_copy(j).wait_recv()
        store(j).wait()
    gw_store.wait()


def leave_kernel(a_hbm, b_hbm, a_out, b_out, a_held, b_held, sems):
    parts = [(b_hbm, b_held, b_out)]
    step = a_hbm.shape[1] // 2
    for r in range(a_hbm.shape[0]):
        for i in range(2):
            at = (r, pl.ds(i * step, step))
            parts.append((a_hbm.at[at], a_held.at[at], a_out.at[at]))
    first = [pltpu.make_async_copy(p[0], p[1], sems.at[0, i]) for i, p in enumerate(parts)]
    second = [pltpu.make_async_copy(p[1], p[2], sems.at[1, i]) for i, p in enumerate(parts)]
    for c in first:
        c.start()
    for c, then in zip(first, second):
        c.wait()
        then.start()
    for c in second:
        c.wait()


def leave(a, b):
    return pl.pallas_call(
        leave_kernel,
        in_specs=[pl.BlockSpec(memory_space=pl.ANY)] * 2,
        out_specs=[pl.BlockSpec(memory_space=pl.ANY)] * 2,
        out_shape=[jax.ShapeDtypeStruct(t.shape, t.dtype) for t in (a, b)],
        scratch_shapes=[pltpu.VMEM(t.shape, t.dtype) for t in (a, b)]
        + [pltpu.SemaphoreType.DMA((2, 1 + 2 * a.shape[0]))],
    )(a, b)


def local(x, w_qkv, g):
    records, rows, width = x.shape
    streams, blocks = lax.axis_size("stream"), lax.axis_size("tm")
    devices = streams * blocks
    count = devices.bit_length() - 1
    cols = width // GROUPS
    total_frames = records * rows * devices
    part = pltpu.VMEM((GROUPS, 3, *([2] * count), width // devices, cols), jnp.bfloat16)
    tiles = pltpu.VMEM((GROUPS, rows, cols), jnp.bfloat16)
    dma = lambda *shape: pltpu.SemaphoreType.DMA(shape)
    half = lambda *shape: pltpu.VMEM(shape, jnp.bfloat16)
    grad_w, grad_in = pl.pallas_call(
        functools.partial(fused_kernel, float(total_frames) ** (-0.5)),
        in_specs=[pl.BlockSpec(memory_space=pl.ANY)] * 3,
        out_specs=[pl.BlockSpec(memory_space=pl.ANY)] * 2,
        out_shape=(
            jax.ShapeDtypeStruct((width // devices, 3 * width), jnp.float32),
            jax.ShapeDtypeStruct((records, rows, width), jnp.bfloat16),
        ),
        scratch_shapes=[
            half(width, 3 * width),
            half(3 * rows, width),
            half(2, rows, width),
            half(3 * rows, 3 * width),
            half(3 * rows, 3 * width),
            pltpu.VMEM((2, GROUPS, rows, cols), jnp.float32),
            tiles,
            tiles,
            tiles,
            tiles,
            pltpu.VMEM((width // devices, 3 * width), jnp.float32),
            part,
            part,
            dma(3 * GROUPS + 2),
            dma(PIECES),
            dma(PIECES),
            dma(GROUPS),
            dma(GROUPS),
            dma(PIECES),
            dma(PIECES),
            dma(GROUPS),
            dma(GROUPS),
            dma(GROUPS),
            dma(GROUPS),
            dma(GROUPS),
            dma(GROUPS, 3),
            dma(GROUPS, 3, count),
        ],
        compiler_params=pltpu.CompilerParams(
            collective_id=0, has_side_effects=True, vmem_limit_bytes=60 << 20
        ),
        cost_estimate=pl.CostEstimate(
            flops=32 * records * rows * width * width,
            bytes_accessed=6 * w_qkv.size,
            transcendentals=4 * HEADS * rows * rows,
        ),
    )(x, w_qkv, g)
    return tuple(leave(grad_in, grad_w))


def solution(mesh):
    return jax.shard_map(
        local,
        mesh=mesh,
        in_specs=(P("stream", "tm", None), P(), P("stream", "tm", None)),
        out_specs=(P("stream", "tm", None), P(("stream", "tm"), None)),
        check_vma=False,
    )
```

```python
import functools

import jax
import jax.numpy as jnp
from jax import lax
from jax.experimental import pallas as pl
from jax.experimental.pallas import tpu as pltpu
from jax.sharding import PartitionSpec as P

HEADS = 8
TOGETHER = 2
GROUPS = HEADS // TOGETHER
PIECES = 6
EARLY = 4
LOG2E = 1.4426950408889634
NN = (((1,), (0,)), ((), ()))
NT = (((1,), (1,)), ((), ()))
TN = (((0,), (0,)), ((), ()))
MESH = pl.DeviceIdType.MESH


def dot(a, b, dims=NN):
    return lax.dot_general(a, b, dims, preferred_element_type=jnp.float32)


def bit_of(index, bit):
    return (index // (1 << bit)) % 2


def aligned(start, size):
    return pl.ds(pl.multiple_of(start, size), size)


def fused_kernel(
    norm,
    x_hbm,
    w_hbm,
    g_hbm,
    gw_hbm,
    gi_hbm,
    w,
    fr,
    gr,
    qkv,
    d,
    sums,
    back_out,
    back_in,
    ret,
    mine,
    gw,
    held,
    landed,
    load_sem,
    x_send,
    x_recv,
    g_send,
    g_recv,
    halo_send,
    halo_recv,
    back_send,
    back_recv,
    ret_send,
    ret_recv,
    store_sem,
    rs_send,
    rs_recv,
):
    _, rows, width = x_hbm.shape
    head = width // HEADS
    cols = TOGETHER * head
    pairs = 2 * cols
    scale = head ** (-0.5)
    streams, blocks = lax.axis_size("stream"), lax.axis_size("tm")
    stream, block = lax.axis_index("stream"), lax.axis_index("tm")
    side, place, places = block % 2, block // 2, blocks // 2
    other = 1 - side
    has_before, has_after = place > 0, place < places - 1
    stream_bits, block_bits = streams.bit_length() - 1, blocks.bit_length() - 1

    dims = [("stream", b, bit_of(stream, b)) for b in reversed(range(stream_bits))]
    dims += [("tm", b, bit_of(block, b)) for b in reversed(range(block_bits))]
    count = len(dims)
    core = stream_bits - 1
    far = list(reversed(range(core)))
    pair = count - 1
    along = list(reversed(range(stream_bits, count - 1)))
    order_a = [core] + far + along + [pair]
    order_c = [core, pair] + far + along
    order_e = [core] + far + [pair] + along
    orders = [
        [order_e, order_e, order_c],
        [order_e, order_c, order_e],
        [order_c, order_e, order_c],
        [order_a, order_c, order_a],
    ]

    def partner(k):
        axis, b, value = dims[k]
        return {axis: (stream if axis == "stream" else block) + (1 - 2 * value) * (1 << b)}

    beside = {"tm": block + 1 - 2 * side}
    after, before = {"tm": block + 2}, {"tm": block - 2}

    def remote(src, dst, send, recv, to):
        return pltpu.make_async_remote_copy(
            src_ref=src, dst_ref=dst, send_sem=send, recv_sem=recv, device_id=to, device_id_type=MESH
        )

    loads = []

    def load(src, dst):
        c = pltpu.make_async_copy(src, dst, load_sem.at[len(loads)])
        c.start()
        loads.append(c)
        return c

    piece = rows // PIECES

    def x_copy(i):
        return remote(
            x_hbm.at[other, pl.ds(i * piece, piece)],
            fr.at[aligned((1 + side) * rows + i * piece, piece)],
            x_send.at[i],
            x_recv.at[i],
            beside,
        )

    def g_copy(g):
        span = pl.ds(g * cols, cols)
        return remote(g_hbm.at[other, :, span], gr.at[side, :, span], g_send.at[g], g_recv.at[g], beside)

    def halo_copy(i):
        return remote(
            fr.at[pl.ds(2 * rows + i * piece, piece)],
            fr.at[pl.ds(i * piece, piece)],
            halo_send.at[i],
            halo_recv.at[i],
            after,
        )

    def back_copy(j):
        return remote(back_out.at[j], back_in.at[j], back_send.at[j], back_recv.at[j], before)

    def ret_copy(j):
        span = pl.ds(j * cols, cols)
        return remote(ret.at[j], gi_hbm.at[side, :, span], ret_send.at[j], ret_recv.at[j], beside)

    def project(slot, start, low=0, high=PIECES):
        into = pl.ds(pl.multiple_of(slot * rows + low * piece, piece), (high - low) * piece)

        def body(j, carry):
            span = aligned(start + j * width, width)
            qkv[into, span] = dot(fr[into, :], w[:, span]).astype(qkv.dtype)
            return carry

        lax.fori_loop(0, (3 * width - start) // width, body, 0)

    def attend(b, g):
        keys = pl.ds(pl.multiple_of(b * rows, rows), 2 * rows)
        queries = aligned((b + 1) * rows, rows)
        bias = jnp.where(b + place > 0, 0.0, -1e30).astype(jnp.float32)
        factor = scale * LOG2E
        def at(start):
            return pl.ds(pl.multiple_of(start, head), head)

        for t in range(TOGETHER):
            for_q = at(g * cols + t * head)
            for_k = at(width + g * pairs + t * head)
            for_v = at(width + g * pairs + cols + t * head)
            q, k, v, go = qkv[queries, for_q], qkv[keys, for_k], qkv[keys, for_v], gr[b, :, for_q]
            s = dot(q, k, NT)
            s_prev, s_own = s[:, :rows], s[:, rows:]
            peak = jnp.maximum(
                jnp.max(s_own, 1, keepdims=True), jnp.max(s_prev, 1, keepdims=True) + bias
            )
            shift = peak * factor
            e_prev = jnp.exp2(s_prev * factor - (shift - bias * factor))
            e_own = jnp.exp2(s_own * factor - shift)
            e = jnp.concatenate([e_prev, e_own], 1)
            inverse = 1.0 / jnp.sum(e, 1, keepdims=True)
            dp = dot(go, v, NT)
            delta = jnp.sum(e * dp, 1, keepdims=True) * inverse
            p = e * inverse
            ds = (p * (dp - delta)).astype(jnp.bfloat16)
            pb = p.astype(jnp.bfloat16)
            d[queries, for_q] = (dot(ds, k) * scale).astype(d.dtype)
            for span, terms in ((for_k, dot(ds, q, TN) * scale), (for_v, dot(pb, go, TN))):
                d[keys, span] = (d[keys, span].astype(jnp.float32) + terms).astype(d.dtype)

    def region(g, c, phase, kept):
        order = orders[g][c] if phase else [core]
        index = [slice(None)] * count
        for k in order[:phase]:
            index[k] = dims[k][2]
        last = order[phase]
        index[last] = dims[last][2] if kept else 1 - dims[last][2]
        return (g, c, *index)

    def rs_copy(g, c, phase):
        return remote(
            held.at[region(g, c, phase, False)],
            landed.at[region(g, c, phase, True)],
            rs_send.at[g, c],
            rs_recv.at[g, c, phase],
            partner(orders[g][c][phase] if phase else core),
        )

    def reduce(g, c, phase):
        rs_copy(g, c, phase).wait_recv()
        kept, arrived = region(g, c, phase, True), region(g, c, phase, False)
        total = held[kept].astype(jnp.float32) + landed[arrived].astype(jnp.float32)
        if phase + 1 < count:
            held[kept] = total.astype(held.dtype)
            rs_copy(g, c, phase).wait_send()
            rs_copy(g, c, phase + 1).start()
        else:
            start = c * width + g * cols
            gw[:, start : start + cols] = total * norm

    def weigh(g):
        shape = held.shape[2:]
        at = pl.ds(pl.multiple_of(width + g * pairs, pairs), pairs)
        total = dot(fr[...], d[:, at], TN).astype(held.dtype)
        for c in (1, 2):
            held[g, c] = total[:, (c - 1) * cols : c * cols].reshape(shape)
            rs_copy(g, c, 0).start()
        total = dot(fr[rows:, :], d[rows:, aligned(g * cols, cols)], TN).astype(held.dtype)
        held[g, 0] = total.reshape(shape)
        rs_copy(g, 0, 0).start()

    def back_terms():
        half = 2 * cols

        def body(i, carry):
            terms = dot(d[:rows, width:], w[aligned(i * half, half), width:], NT).astype(back_out.dtype)
            for j in range(2):
                back_out[2 * i + j] = terms[:, j * cols : (j + 1) * cols]
            return carry

        lax.fori_loop(0, GROUPS // 2, body, 0)

    def send_back(j):
        pl.when(has_before)(back_copy(j).start)

    def input_terms(b, into):
        at = aligned((b + 1) * rows, rows)

        half = 2 * cols

        def body(i, carry):
            terms = dot(d[at, :], w[aligned(i * half, half), :], NT)
            for j in range(2):
                sums[into, 2 * i + j] = terms[:, j * cols : (j + 1) * cols]
            return carry

        lax.fori_loop(0, GROUPS // 2, body, 0)

    def add_back(into, j):
        back_copy(j).wait_recv()
        sums[into, j] += back_in[j].astype(jnp.float32)

    def store(j):
        span = pl.ds(j * cols, cols)
        return pltpu.make_async_copy(mine.at[j], gi_hbm.at[side, :, span], store_sem.at[j])

    for g in range(GROUPS):
        for c in range(3):
            load(
                w_hbm.at[:, pl.ds(c * width + g * cols, cols)],
                w.at[:, pl.ds(g * cols if c == 0 else width + g * pairs + (c - 1) * cols, cols)],
            )
    x_load = load(x_hbm.at[side], fr.at[aligned((1 + side) * rows, rows)])
    g_load = load(g_hbm.at[side], gr.at[side])
    barrier = pltpu.get_barrier_semaphore()

    def greet(to):
        pl.semaphore_signal(barrier, inc=1, device_id=to, device_id_type=MESH)

    for k in range(count):
        greet(partner(k))
    pl.when(has_before)(lambda: greet(before))
    pl.when(has_after)(lambda: greet(after))
    near = (place + places - 1) // places + (2 * places - 2 - place) // places
    pl.semaphore_wait(barrier, count + near)

    for i in range(PIECES):
        x_copy(i).start()
    for g in range(GROUPS):
        g_copy(g).start()
    d[...] = jnp.zeros_like(d)

    @pl.when(jnp.logical_not(has_before))
    def _():
        fr[:rows] = jnp.zeros((rows, width), fr.dtype)

    x_load.wait()

    @pl.when(jnp.logical_and(side == 1, has_after))
    def _():
        for i in range(PIECES):
            halo_copy(i).start()

    for c in loads[: 3 * GROUPS]:
        c.wait()
    project(1 + side, 0)
    for i in range(PIECES):
        x_copy(i).wait_recv()
        pl.when(jnp.logical_and(side == 0, has_after))(halo_copy(i).start)
        if i == EARLY - 1:
            project(1 + other, 0, 0, EARLY)
    project(1 + other, 0, EARLY, PIECES)
    g_load.wait()

    def meet(g):
        g_copy(g).wait_recv()

    def halo():
        @pl.when(has_before)
        def _():
            for i in range(PIECES):
                halo_copy(i).wait_recv()

        project(0, width)

    def give(j):
        ret[j] = sums[0, j].astype(ret.dtype)
        ret_copy(j).start()

    def give_soon():
        for j in range(GROUPS):
            give(j)

    def give_late(j):
        @pl.when(side == 0)
        def _():
            pl.when(has_after)(functools.partial(add_back, 0, j))
            give(j)

    def keep(j):
        pl.when(jnp.logical_and(side == 1, has_after))(functools.partial(add_back, 1, j))
        mine[j] = sums[1, j].astype(mine.dtype)
        store(j).start()

    def reduce_all(g, phase):
        for c in range(3):
            reduce(g, c, phase)

    turns = ((0, 0), (1, 0), (0, 1), (1, 1), (0, 2), (0, 3), (1, 2), (1, 3))
    block_table = sum(b << i for i, (b, _) in enumerate(turns))
    group_table = sum(g << (2 * i) for i, (_, g) in enumerate(turns))

    def turn(i, carry):
        b = ((block_table >> i) + side * ((3 >> i) % 2)) % 2
        g = (group_table >> (2 * i)) % GROUPS

        pl.when(jnp.logical_and(i == 0, side == 0))(halo)
        for at, arriving in ((1, 0), (2, 1), (4, 2), (5, 3)):
            pl.when(i == at)(functools.partial(meet, arriving))
        attend(b, g)

        pl.when(jnp.logical_and(i == 0, side == 1))(halo)

        @pl.when(i == 4)
        def _():
            reduce_all(0, 1)

        @pl.when(i == 5)
        def _():
            back_terms()
            send_back(0)
            send_back(1)
            reduce_all(1, 1)

        @pl.when(i == 6)
        def _():
            reduce_all(0, 2)
            send_back(2)
            send_back(3)

        @pl.when(jnp.logical_or(i == 1, jnp.logical_or(i == 3, i == 6)))
        def _():
            weigh(g)

        for at, group in ((1, 0), (3, 1), (6, 2)):
            pl.when(i == at)(functools.partial(reduce_all, group, 0))
        return carry

    lax.fori_loop(0, len(turns), turn, 0)
    done = [[3] * 3, [2] * 3, [1] * 3, [0] * 3]

    def step(g, ready=(0, 1, 2)):
        for c in ready:
            if done[g][c] < count:
                reduce(g, c, done[g][c])
                done[g][c] += 1

    def slant(g):
        ahead = [True, done[g][0] - done[g][1] >= 1, done[g][1] - done[g][2] >= 1]
        full = [n >= count - 1 for n in done[g]]
        ready = [c for c in (2, 1, 0) if ahead[c] or (c and full[c - 1])]
        step(g, [c for c in ready if not full[c]])

    step(1)
    input_terms(other, 0)
    pl.when(side == 1)(functools.partial(give, 0))
    give_late(0)
    pl.when(side == 1)(functools.partial(give, 1))
    weigh(3)
    step(3)
    give_late(1)
    step(2)
    step(0)
    input_terms(side, 1)
    pl.when(side == 1)(functools.partial(give, 2))
    give_late(2)
    slant(3)
    pl.when(side == 1)(functools.partial(give, 3))
    slant(3)
    give_late(3)
    step(1)
    slant(3)
    step(2)
    slant(3)
    step(2)
    slant(3)
    step(0)
    step(1)
    for j in range(GROUPS):
        keep(j)
    for _ in range(count):
        for g in range(GROUPS):
            slant(g)
    for g in range(GROUPS):
        step(g)

    gw_store = pltpu.make_async_copy(gw, gw_hbm, load_sem.at[0])
    gw_store.start()

    for i in range(PIECES):
        x_copy(i).wait_send()
    for g in range(GROUPS):
        g_copy(g).wait_send()
        for c in range(3):
            rs_copy(g, c, count - 1).wait_send()

    @pl.when(has_after)
    def _():
        for i in range(PIECES):
            halo_copy(i).wait_send()

    @pl.when(has_before)
    def _():
        for j in range(GROUPS):
            back_copy(j).wait_send()

    for j in range(GROUPS):
        ret_copy(j).wait_send()
        ret_copy(j).wait_recv()
        store(j).wait()
    gw_store.wait()


def leave_kernel(a_hbm, b_hbm, a_out, b_out, a_held, b_held, sems):
    parts = [(b_hbm, b_held, b_out)]
    split = 4
    step = a_hbm.shape[1] // split
    for r in range(a_hbm.shape[0]):
        for i in range(split):
            at = (r, pl.ds(i * step, step))
            parts.append((a_hbm.at[at], a_held.at[at], a_out.at[at]))
    first = [pltpu.make_async_copy(p[0], p[1], sems.at[0, i]) for i, p in enumerate(parts)]
    second = [pltpu.make_async_copy(p[1], p[2], sems.at[1, i]) for i, p in enumerate(parts)]
    for c in first:
        c.start()
    for c, then in zip(first, second):
        c.wait()
        then.start()
    for c in second:
        c.wait()


def leave(a, b):
    return pl.pallas_call(
        leave_kernel,
        in_specs=[pl.BlockSpec(memory_space=pl.ANY)] * 2,
        out_specs=[pl.BlockSpec(memory_space=pl.ANY)] * 2,
        out_shape=[jax.ShapeDtypeStruct(t.shape, t.dtype) for t in (a, b)],
        scratch_shapes=[pltpu.VMEM(t.shape, t.dtype) for t in (a, b)]
        + [pltpu.SemaphoreType.DMA((2, 1 + 4 * a.shape[0]))],
    )(a, b)


def local(x, w_qkv, g):
    records, rows, width = x.shape
    streams, blocks = lax.axis_size("stream"), lax.axis_size("tm")
    devices = streams * blocks
    count = devices.bit_length() - 1
    cols = width // GROUPS
    total_frames = records * rows * devices
    part = pltpu.VMEM((GROUPS, 3, *([2] * count), width // devices, cols), jnp.bfloat16)
    tiles = pltpu.VMEM((GROUPS, rows, cols), jnp.bfloat16)
    dma = lambda *shape: pltpu.SemaphoreType.DMA(shape)
    half = lambda *shape: pltpu.VMEM(shape, jnp.bfloat16)
    grad_w, grad_in = pl.pallas_call(
        functools.partial(fused_kernel, float(total_frames) ** (-0.5)),
        in_specs=[pl.BlockSpec(memory_space=pl.ANY)] * 3,
        out_specs=[pl.BlockSpec(memory_space=pl.ANY)] * 2,
        out_shape=(
            jax.ShapeDtypeStruct((width // devices, 3 * width), jnp.float32),
            jax.ShapeDtypeStruct((records, rows, width), jnp.bfloat16),
        ),
        scratch_shapes=[
            half(width, 3 * width),
            half(3 * rows, width),
            half(2, rows, width),
            half(3 * rows, 3 * width),
            half(3 * rows, 3 * width),
            pltpu.VMEM((2, GROUPS, rows, cols), jnp.float32),
            tiles,
            tiles,
            tiles,
            tiles,
            pltpu.VMEM((width // devices, 3 * width), jnp.float32),
            part,
            part,
            dma(3 * GROUPS + 2),
            dma(PIECES),
            dma(PIECES),
            dma(GROUPS),
            dma(GROUPS),
            dma(PIECES),
            dma(PIECES),
            dma(GROUPS),
            dma(GROUPS),
            dma(GROUPS),
            dma(GROUPS),
            dma(GROUPS),
            dma(GROUPS, 3),
            dma(GROUPS, 3, count),
        ],
        compiler_params=pltpu.CompilerParams(
            collective_id=0, has_side_effects=True, vmem_limit_bytes=60 << 20
        ),
        cost_estimate=pl.CostEstimate(
            flops=32 * records * rows * width * width,
            bytes_accessed=6 * w_qkv.size,
            transcendentals=4 * HEADS * rows * rows,
        ),
    )(x, w_qkv, g)
    return tuple(leave(grad_in, grad_w))


def solution(mesh):
    return jax.shard_map(
        local,
        mesh=mesh,
        in_specs=(P("stream", "tm", None), P(), P("stream", "tm", None)),
        out_specs=(P("stream", "tm", None), P(("stream", "tm"), None)),
        check_vma=False,
    )
```
